32 devices in a mesh: dp: 16 (over z, y, core), tensor: 2 (over x).
Axes of the slice: x: 2, y: 2, z: 4, core: 2. Of those that a mesh axis runs over, the one named last changes fastest.
Arguments:
- block_input: bfloat16 [4096, 2048], P('dp'), may hold values from -6 to 6
- cotangent: float32 [4096, 2048], P('dp'), may hold values from -6 to 6
- seq_lengths: int32 [16, 4], P('dp'), may hold values from 0 to 256, as said below
- norm_attn_gain: float32 [2048], replicated, may hold values from 0.5 to 1.5
- norm_attn_shift: float32 [2048], replicated, may hold values from -1.5 to 1.5
- norm_mlp_gain: float32 [2048], replicated, may hold values from 0.5 to 1.5
- norm_mlp_shift: float32 [2048], replicated, may hold values from -1.5 to 1.5
- w_query: bfloat16 [2048, 2048], P('dp', 'tensor')
- w_key: bfloat16 [2048, 2048], P('dp', 'tensor')
- w_value: bfloat16 [2048, 2048], P('dp', 'tensor'), may hold values from -0.125 to 0.125
- query_bias: float32 [2048], P('tensor'), may hold values from -2.5 to 2.5
- key_bias: float32 [8, 64], P('tensor'), may hold values from -2.5 to 2.5
- value_bias: float32 [2048], P('tensor'), may hold values from -2.5 to 2.5
- w_attn_out: bfloat16 [2048, 2048], P('tensor', 'dp'), may hold values from -1.5 to 1.5
- attn_out_bias: float32 [2048], replicated, may hold values from -1.5 to 1.5
- w_up: bfloat16 [2048, 8192], P('dp', 'tensor'), may hold values from -0.125 to 0.125
- up_bias: float32 [8192], P('tensor'), may hold values from -2.5 to 2.5
- w_down: bfloat16 [8192, 2048], P('tensor', 'dp'), may hold values from -0.0625 to 0.0625
- down_bias: float32 [2048], replicated, may hold values from -1.5 to 1.5
Outputs:
- block_output: float32 [4096, 2048], P('dp')
- input_grad: float32 [4096, 2048], P('dp')
- grad_norm_attn_gain: float32 [2048], replicated
- grad_norm_attn_shift: float32 [2048], replicated
- grad_norm_mlp_gain: float32 [2048], replicated
- grad_norm_mlp_shift: float32 [2048], replicated
- grad_w_query: float32 [2048, 2048], P('dp', 'tensor')
- grad_w_key: float32 [2048, 2048], P('dp', 'tensor')
- grad_w_value: float32 [2048, 2048], P('dp', 'tensor')
- grad_query_bias: float32 [2048], P('tensor')
- grad_key_bias: float32 [8, 64], P('tensor')
- grad_value_bias: float32 [2048], P('tensor')
- grad_w_attn_out: float32 [2048, 2048], P('tensor', 'dp')
- grad_attn_out_bias: float32 [2048], replicated
- grad_w_up: float32 [2048, 8192], P('dp', 'tensor')
- grad_up_bias: float32 [8192], P('tensor')
- grad_w_down: float32 [8192, 2048], P('tensor', 'dp')
- grad_down_bias: float32 [2048], replicated
The draws below stay inside these ranges and needn't reach their ends.
Inputs may be any that keep to these rules, and one draw needn't show every extreme that they name: `seq_lengths`: in each row the nonzero lengths come first; each sequence fills whole padding blocks except for its last one; the lengths of a row rounded up to multiples of 128 sum to at most 256; some row holds a single sequence of 256 tokens.
All inputs are finite; a program needn't handle non-finite values.
Results may differ from the reference program's by a relative error of at most 0.025.
Values may be sent and summed in bfloat16 or wider, within the bound.
No kernel may reach another device: no remote copies, remote signals or barrier semaphores. Data moves between devices by JAX's collectives and lax.ppermute only.
A program may use at most 256 MiB of HBM per device.

```python
import math
import jax
import jax.numpy as jnp
from jax import lax

D = 2048
HEADS = 8
HEAD_DIM = 256
ROT = 64
FF = 8192
TOK_DEV = 256
SEQ_DEV = 4
BLOCK = 128
DATA_SHARDS = 16
TOKENS = 4096


def query_base(key):
    return jax.random.normal(jax.random.fold_in(key, 101), (D, D), jnp.float32) * D ** (-0.5)


def draw_w_query(key, part):
    return query_base(key).astype(jnp.bfloat16)


def draw_w_key(key, part):
    own_part = jax.random.normal(jax.random.fold_in(key, 202), (D, D), jnp.float32) * D ** (-0.5)
    return own_part.astype(jnp.bfloat16)


def draw_seq_lengths(key, part):
    blocks_dev = TOK_DEV // BLOCK
    key_live, key_start, key_cut, key_full = jax.random.split(jax.random.fold_in(key, 303), 4)
    shard_index = jnp.arange(DATA_SHARDS, dtype=jnp.int32)
    full_shard = jax.random.randint(key_full, (), 0, DATA_SHARDS)
    is_full = shard_index == full_shard
    live = jax.random.randint(key_live, (DATA_SHARDS,), 1, blocks_dev + 1)
    live = jnp.where(is_full, blocks_dev, live)
    block_index = jnp.arange(blocks_dev, dtype=jnp.int32)
    new_seq = jax.random.randint(key_start, (DATA_SHARDS, blocks_dev), 0, 2)
    new_seq = jnp.where((block_index[None, :] == 0) | is_full[:, None], 0, new_seq)
    which = jnp.minimum(jnp.cumsum(new_seq, axis=1), SEQ_DEV - 1)
    used = block_index[None, :] < live[:, None]
    slot_index = jnp.arange(SEQ_DEV, dtype=jnp.int32)
    member = (which[:, :, None] == slot_index[None, None, :]) & used[:, :, None]
    counts = jnp.sum(member.astype(jnp.int32), axis=1)
    cut = jax.random.randint(key_cut, (DATA_SHARDS, SEQ_DEV), 0, BLOCK)
    cut = jnp.where(is_full[:, None], 0, cut)
    return jnp.where(counts > 0, counts * BLOCK - cut, 0).astype(jnp.int32)


def raised(drawn, stream_key, source, target, parts, factor):
    owner, partner = [(jnp.arange(drawn.shape[dim]) // (drawn.shape[dim] // parts)).reshape([-1 if axis == dim else 1 for axis in range(drawn.ndim)]) for dim in (source, target)]
    chosen = jax.random.permutation(stream_key, parts)[partner]
    strong = (owner == chosen) | (owner == (partner + parts // 2) % parts)
    return jnp.where(strong, factor * drawn, drawn)


def steps_of(key, extent, cuts, smallest, largest):
    def one(dim, blocks):
        draws = jax.random.uniform(jax.random.fold_in(jax.random.fold_in(key, 6), dim), (blocks,), jnp.float32, smallest / len(cuts), largest / len(cuts))
        return jnp.repeat(jnp.exp(draws), extent[dim] // blocks).reshape((-1,) + (1,) * (len(extent) - dim - 1))

    level = one(*cuts[0])
    for cut in cuts[1:]:
        level = level * one(*cut)
    return level


def centred(own_key, extent, deviation, most, pieces=(), kind=jnp.bfloat16):
    level = steps_of(own_key, extent, pieces, -0.22, 0.18) if pieces else 1.0
    drawn = jax.random.normal(own_key, extent, jnp.float32) * deviation * level
    return jnp.minimum(jnp.maximum(drawn, -most), most).astype(kind)


def heavy_noise(key, extent, deviation, bound, cuts, heavy, kind=jnp.bfloat16):
    drawn = deviation * jax.random.normal(key, extent, jnp.float32)
    if cuts:
        drawn = drawn * steps_of(key, extent, cuts, -0.22, 0.18)
    return jnp.clip(raised(drawn, jax.random.fold_in(key, 3), *heavy), -bound, bound).astype(kind)


def setup_inputs(seed: int = 0) -> dict:
    seeds = jax.random.split(jax.random.key(seed), 20)
    block_input = heavy_noise(seeds[0], (TOKENS, D), 1.0, 6.0, ((0, 16),), (0, 1, 16, 2.0))
    cotangent = heavy_noise(seeds[1], (TOKENS, D), 1.0, 6.0, ((0, 16),), (0, 1, 16, 2.0), jnp.float32)
    seq_lengths = draw_seq_lengths(jax.random.fold_in(seeds[19], 71), 0)
    norm_attn_gain = jnp.clip(1.0 + 0.1 * jax.random.normal(seeds[3], (D,), jnp.float32), 0.5, 1.5)
    norm_attn_shift = centred(seeds[4], (D,), 0.3, 1.5, (), jnp.float32)
    norm_mlp_gain = jnp.clip(1.0 + 0.1 * jax.random.normal(seeds[5], (D,), jnp.float32), 0.5, 1.5)
    norm_mlp_shift = centred(seeds[6], (D,), 0.3, 1.5, (), jnp.float32)
    w_query = draw_w_query(jax.random.fold_in(seeds[19], 71), 0)
    w_key = draw_w_key(jax.random.fold_in(seeds[19], 71), 0)
    w_value = centred(seeds[9], (D, D), D ** -0.5, 0.125, ((0, 16), (1, 2)))
    query_bias = centred(seeds[10], (D,), 0.5, 2.5, ((0, 2),), jnp.float32)
    key_bias = centred(seeds[11], (HEADS, ROT), 0.5, 2.5, ((0, 2),), jnp.float32)
    value_bias = centred(seeds[12], (D,), 0.5, 2.5, ((0, 2),), jnp.float32)
    w_attn_out = centred(seeds[13], (D, D), (max(D // 128, 1)) ** -0.5, 1.5, ((0, 2), (1, 16)))
    attn_out_bias = centred(seeds[14], (D,), 0.3, 1.5, (), jnp.float32)
    w_up = centred(seeds[15], (D, FF), D ** -0.5, 0.125, ((0, 16), (1, 2)))
    up_bias = centred(seeds[16], (FF,), 0.5, 2.5, ((0, 2),), jnp.float32)
    w_down = centred(seeds[17], (FF, D), FF ** -0.5, 0.0625, ((0, 2), (1, 16)))
    down_bias = centred(seeds[18], (D,), 0.3, 1.5, (), jnp.float32)
    return {"block_input": block_input, "cotangent": cotangent, "seq_lengths": seq_lengths, "norm_attn_gain": norm_attn_gain, "norm_attn_shift": norm_attn_shift, "norm_mlp_gain": norm_mlp_gain, "norm_mlp_shift": norm_mlp_shift, "w_query": w_query, "w_key": w_key, "w_value": w_value, "query_bias": query_bias, "key_bias": key_bias, "value_bias": value_bias, "w_attn_out": w_attn_out, "attn_out_bias": attn_out_bias, "w_up": w_up, "up_bias": up_bias, "w_down": w_down, "down_bias": down_bias}


EPSILON = 1e-05
ROOT_HALF = 0.7071067811865476
DENSITY_SCALE = 0.3989422804014327
MASKED_SCORE = -1e+30

def layout(lengths, tok_count):
    padded_len = (lengths + BLOCK - 1) // BLOCK * BLOCK
    starts = jnp.cumsum(padded_len) - padded_len
    row_index = jnp.arange(tok_count, dtype=jnp.int32)
    inside = (row_index[:, None] >= starts[None, :]) & (row_index[:, None] < (starts + lengths)[None, :])
    number = jnp.arange(lengths.shape[0], dtype=jnp.int32)
    segment = lax.optimization_barrier(jnp.sum(jnp.where(inside, number[None, :] + 1, 0), axis=1)) - 1
    position = lax.optimization_barrier(jnp.sum(jnp.where(inside, row_index[:, None] - starts[None, :], 0), axis=1))
    half_rot = ROT // 2
    frequency = 10000.0 ** (-(2.0 * jnp.arange(half_rot, dtype=jnp.float32)) / ROT)
    angles = position.astype(jnp.float32)[:, None] * frequency[None, :]
    same_seq = (segment[:, None] == segment[None, :]) & (segment[:, None] >= 0)
    diagonal = row_index[:, None] == row_index[None, :]
    allowed = (row_index[None, :] <= row_index[:, None]) & (same_seq | diagonal)
    return (jnp.cos(angles), jnp.sin(angles), allowed)

def rotate(values, cosine_rows, sine_rows):
    half_rot = cosine_rows.shape[1]
    front_half = values[:, :, :half_rot]
    back_half = values[:, :, half_rot:2 * half_rot]
    cos_heads = cosine_rows[:, None, :]
    sin_heads = sine_rows[:, None, :]
    return jnp.concatenate([front_half * cos_heads - back_half * sin_heads, back_half * cos_heads + front_half * sin_heads, values[:, :, 2 * half_rot:]], axis=2)

def norm_forward(source, gain, shift):
    center = source - lax.optimization_barrier(jnp.mean(source, axis=1, keepdims=True))
    inv_scale = lax.rsqrt(lax.optimization_barrier(jnp.mean(center * center, axis=1, keepdims=True)) + EPSILON)
    normed = center * inv_scale
    return (normed * gain + shift, normed, inv_scale)

def norm_backward(grad_out, normed, inv_scale, gain):
    gain_grad = lax.optimization_barrier(jnp.sum(grad_out * normed, axis=0))
    shift_grad = lax.optimization_barrier(jnp.sum(grad_out, axis=0))
    grad_normed = grad_out * gain
    grad_input = inv_scale * (grad_normed - lax.optimization_barrier(jnp.mean(grad_normed, axis=1, keepdims=True)) - normed * lax.optimization_barrier(jnp.mean(grad_normed * normed, axis=1, keepdims=True)))
    return (grad_input, gain_grad, shift_grad)

def gelu_value(inputs):
    return 0.5 * inputs * (1.0 + lax.erf(inputs * ROOT_HALF))

def gelu_slope(inputs):
    return 0.5 * (1.0 + lax.erf(inputs * ROOT_HALF)) + inputs * jnp.exp(-0.5 * inputs * inputs) * DENSITY_SCALE

def product(factor, second):
    return jnp.dot(factor, second, preferred_element_type=jnp.float32)

def inner_rows(factor, second):
    return lax.dot_general(factor, second, (((0,), (0,)), ((), ())), preferred_element_type=jnp.float32)

def outer_rows(factor, second):
    return lax.dot_general(factor, second, (((1,), (1,)), ((), ())), preferred_element_type=jnp.float32)

def score_block(query_rot, key_rot, allowed):
    scores = jnp.einsum('qhd,khd->hqk', query_rot.astype(jnp.float32), key_rot.astype(jnp.float32)) * (1.0 / math.sqrt(HEAD_DIM))
    return jnp.where(allowed[None, :, :], scores, MASKED_SCORE)

def whole_layer(block_rows, grad_out, lengths, norms, weights, biases, out_biases):
    norm_attn_gain, norm_attn_shift, norm_mlp_gain, norm_mlp_shift = norms
    w_query, w_key, w_value, w_attn_out, w_up, w_down = weights
    query_bias, key_bias, value_bias, up_bias = biases
    attn_out_bias, down_bias = out_biases
    tok_count = block_rows.shape[0]
    heads_all = w_query.shape[1] // HEAD_DIM
    head_shape = (tok_count, heads_all, HEAD_DIM)
    cosine_rows, sine_rows, allowed = layout(lengths, tok_count)
    source = block_rows.astype(jnp.float32)
    norm_attn, normed_attn, scale_attn = norm_forward(source, norm_attn_gain, norm_attn_shift)
    norm_mlp, normed_mlp, scale_mlp = norm_forward(source, norm_mlp_gain, norm_mlp_shift)
    attn_in = norm_attn.astype(jnp.bfloat16)
    mlp_in = norm_mlp.astype(jnp.bfloat16)
    query_pre = (product(attn_in, w_query) + query_bias).reshape(head_shape)
    key_pre = product(attn_in, w_key).reshape(head_shape)
    key_pre = key_pre.at[:, :, :ROT].add(key_bias[None, :, :])
    value_pre = product(attn_in, w_value) + value_bias
    query_rot = rotate(query_pre, cosine_rows, sine_rows).astype(jnp.bfloat16)
    key_rot = rotate(key_pre, cosine_rows, sine_rows).astype(jnp.bfloat16)
    value_rows = value_pre.astype(jnp.bfloat16).reshape(head_shape)
    scores = score_block(query_rot, key_rot, allowed)
    row_top = lax.optimization_barrier(jnp.max(scores, axis=2, keepdims=True))
    log_total = row_top + jnp.log(lax.optimization_barrier(jnp.sum(jnp.exp(scores - row_top), axis=2, keepdims=True)))
    probs = jnp.exp(scores - log_total)
    probs_b = probs.astype(jnp.bfloat16)
    attn_rows = jnp.einsum('hqk,khd->qhd', probs_b.astype(jnp.float32), value_rows.astype(jnp.float32))
    attn_rows = attn_rows.astype(jnp.bfloat16).reshape(tok_count, -1)
    up_pre = product(mlp_in, w_up) + up_bias
    activ_rows = gelu_value(up_pre).astype(jnp.bfloat16)
    mixed = product(attn_rows, w_attn_out) + product(activ_rows, w_down)
    block_output = source + mixed + attn_out_bias + down_bias
    grad_rows = grad_out.astype(jnp.bfloat16)
    out_bias_grad = lax.optimization_barrier(jnp.sum(grad_out, axis=0))
    grad_w_down = inner_rows(activ_rows, grad_rows)
    grad_w_out = inner_rows(attn_rows, grad_rows)
    grad_up = outer_rows(grad_rows, w_down) * gelu_slope(up_pre)
    grad_up_bias = lax.optimization_barrier(jnp.sum(grad_up, axis=0))
    grad_up_b = grad_up.astype(jnp.bfloat16)
    grad_w_up = inner_rows(mlp_in, grad_up_b)
    grad_norm_mlp = outer_rows(grad_up_b, w_up)
    grad_attn = outer_rows(grad_rows, w_attn_out).astype(jnp.bfloat16).reshape(head_shape)
    delta = lax.optimization_barrier(jnp.sum(grad_attn.astype(jnp.float32) * attn_rows.reshape(head_shape).astype(jnp.float32), axis=2)).T
    probs_again = jnp.exp(score_block(query_rot, key_rot, allowed) - log_total)
    grad_probs = jnp.einsum('qhd,khd->hqk', grad_attn.astype(jnp.float32), value_rows.astype(jnp.float32))
    grad_scores = (probs_again * (grad_probs - delta[:, :, None])).astype(jnp.bfloat16).astype(jnp.float32)
    score_scale = 1.0 / math.sqrt(HEAD_DIM)
    grad_query = jnp.einsum('hqk,khd->qhd', grad_scores, key_rot.astype(jnp.float32)) * score_scale
    grad_key = jnp.einsum('hqk,qhd->khd', grad_scores, query_rot.astype(jnp.float32)) * score_scale
    grad_value = jnp.einsum('hqk,qhd->khd', probs_b.astype(jnp.float32), grad_attn.astype(jnp.float32))
    grad_query = rotate(grad_query, cosine_rows, -sine_rows)
    grad_key = rotate(grad_key, cosine_rows, -sine_rows)
    grad_query_bias = lax.optimization_barrier(jnp.sum(grad_query, axis=0)).reshape(-1)
    grad_key_bias = lax.optimization_barrier(jnp.sum(grad_key[:, :, :ROT], axis=0))
    grad_value_bias = lax.optimization_barrier(jnp.sum(grad_value, axis=0)).reshape(-1)
    grad_query_b = grad_query.reshape(tok_count, -1).astype(jnp.bfloat16)
    grad_key_b = grad_key.reshape(tok_count, -1).astype(jnp.bfloat16)
    grad_value_b = grad_value.reshape(tok_count, -1).astype(jnp.bfloat16)
    grad_w_query = inner_rows(attn_in, grad_query_b)
    grad_w_key = inner_rows(attn_in, grad_key_b)
    grad_w_value = inner_rows(attn_in, grad_value_b)
    grad_norm_attn = outer_rows(grad_query_b, w_query) + outer_rows(grad_key_b, w_key) + outer_rows(grad_value_b, w_value)
    input_attn, gain_attn, shift_attn = norm_backward(grad_norm_attn, normed_attn, scale_attn, norm_attn_gain)
    input_mlp, gain_mlp, shift_mlp = norm_backward(grad_norm_mlp, normed_mlp, scale_mlp, norm_mlp_gain)
    input_grad = grad_out + input_attn + input_mlp
    grads = (gain_attn, shift_attn, gain_mlp, shift_mlp, grad_w_query, grad_w_key, grad_w_value, grad_query_bias, grad_key_bias, grad_value_bias, grad_w_out, out_bias_grad, grad_w_up, grad_up_bias, grad_w_down, out_bias_grad)
    return (block_output, input_grad, grads)

def add_pair(first_term, second_term):
    return first_term + second_term

def reference(block_input, cotangent, seq_lengths, norm_attn_gain, norm_attn_shift, norm_mlp_gain, norm_mlp_shift, w_query, w_key, w_value, query_bias, key_bias, value_bias, w_attn_out, attn_out_bias, w_up, up_bias, w_down, down_bias):
    shards = seq_lengths.shape[0]
    rows_in = block_input.reshape(shards, -1, D)
    rows_grad = cotangent.reshape(shards, -1, D)
    norms = (norm_attn_gain, norm_attn_shift, norm_mlp_gain, norm_mlp_shift)
    weights = (w_query, w_key, w_value, w_attn_out, w_up, w_down)
    biases = (query_bias, key_bias, value_bias, up_bias)
    out_biases = (attn_out_bias, down_bias)
    params = (norm_attn_gain, norm_attn_shift, norm_mlp_gain, norm_mlp_shift, w_query, w_key, w_value, query_bias, key_bias, value_bias, w_attn_out, attn_out_bias, w_up, up_bias, w_down, down_bias)
    initial = tuple((jnp.zeros(param.shape, jnp.float32) for param in params))

    def shard_step(totals, items):
        block_rows, grad_out, lengths = items
        result, grad_in, grads = whole_layer(block_rows, grad_out, lengths, norms, weights, biases, out_biases)
        return (jax.tree.map(add_pair, totals, grads), (result, grad_in))
    totals, (outputs, grads_in) = lax.scan(shard_step, initial, (rows_in, rows_grad, seq_lengths))
    return (outputs.reshape(-1, D), grads_in.reshape(-1, D), totals[0], totals[1], totals[2], totals[3], totals[4], totals[5], totals[6], totals[7], totals[8], totals[9], totals[10], totals[11], totals[12], totals[13], totals[14], totals[15])
```

```python
import math

import jax
import jax.numpy as jnp
from jax import lax
from jax.sharding import PartitionSpec as P

HEAD_DIM = 256
ROT = 64
BLOCK = 128
GROUP = 4

EPSILON = 1e-05
ROOT_HALF = 0.7071067811865476
DENSITY_SCALE = 0.3989422804014327
MASKED_SCORE = -1e30


BF = jnp.bfloat16
F32 = jnp.float32


def layout(lengths, tok_count):
    padded_len = (lengths + BLOCK - 1) // BLOCK * BLOCK
    starts = jnp.cumsum(padded_len) - padded_len
    row_index = jnp.arange(tok_count, dtype=jnp.int32)
    inside = (row_index[:, None] >= starts[None, :]) & (
        row_index[:, None] < (starts + lengths)[None, :]
    )
    number = jnp.arange(lengths.shape[0], dtype=jnp.int32)
    segment = jnp.sum(jnp.where(inside, number[None, :] + 1, 0), axis=1) - 1
    position = jnp.sum(jnp.where(inside, row_index[:, None] - starts[None, :], 0), axis=1)
    half_rot = ROT // 2
    frequency = 10000.0 ** (-(2.0 * jnp.arange(half_rot, dtype=jnp.float32)) / ROT)
    angles = position.astype(jnp.float32)[:, None] * frequency[None, :]
    same_seq = (segment[:, None] == segment[None, :]) & (segment[:, None] >= 0)
    diagonal = row_index[:, None] == row_index[None, :]
    allowed = (row_index[None, :] <= row_index[:, None]) & (same_seq | diagonal)
    return (jnp.cos(angles), jnp.sin(angles), allowed)


def rotate(values, cosine_rows, sine_rows):
    half_rot = cosine_rows.shape[-1]
    front = values[..., :half_rot]
    back = values[..., half_rot : 2 * half_rot]
    return jnp.concatenate(
        [
            front * cosine_rows - back * sine_rows,
            back * cosine_rows + front * sine_rows,
            values[..., 2 * half_rot :],
        ],
        axis=-1,
    )


def gelu_value(inputs):
    return 0.5 * inputs * (1.0 + lax.erf(inputs * ROOT_HALF))


def gelu_slope(inputs):
    return (
        0.5 * (1.0 + lax.erf(inputs * ROOT_HALF))
        + inputs * jnp.exp(-0.5 * inputs * inputs) * DENSITY_SCALE
    )


def dot(a, b):
    return jnp.dot(a, b, preferred_element_type=F32)


def dot_tn(a, b):
    return lax.dot_general(a, b, (((0,), (0,)), ((), ())), preferred_element_type=F32)


def dot_nt(a, b):
    return lax.dot_general(a, b, (((1,), (1,)), ((), ())), preferred_element_type=F32)


class Links:
    def __init__(self):
        self.n = lax.axis_size("dp")
        self.nz = self.n // GROUP
        d = lax.axis_index("dp")
        self.z, self.y, self.c = d // 4, (d // 2) % 2, d % 2
        if self.nz == 4:
            low = self.z < 2
            self.order = [self.z, self.z ^ 1, jnp.where(low, 2, 1), jnp.where(low, 3, 0)]
        else:
            self.order = [lax.rem(self.z + k, self.nz) for k in range(self.nz)]

    def zperm(self, a, zpairs):
        return lax.ppermute(
            a, "dp", [(4 * s + j, 4 * t + j) for s, t in zpairs for j in range(4)]
        )

    def yswap(self, a):
        return lax.ppermute(a, "dp", [(d, d ^ 2) for d in range(self.n)])

    def cswap(self, a):
        return lax.ppermute(a, "dp", [(d, d ^ 1) for d in range(self.n)])

    def xswap(self, a):
        t = lax.axis_size("tensor")
        return lax.ppermute(a, "tensor", [(i, t - 1 - i) for i in range(t)])

    def pick(self, a, i):
        return lax.dynamic_index_in_dim(a, i, 0, keepdims=False)

    def pair(self, own, other, bit, axis):
        return jnp.where(
            bit == 0, jnp.stack([own, other], axis), jnp.stack([other, own], axis)
        )

    def spread(self, pieces):
        rows, cols = pieces.shape[1:]
        p = pieces.reshape(2, 2, rows, cols)
        got = self.yswap(self.pick(p, 1 - self.y))
        w = self.pair(self.pick(p, self.y), got, self.y, 1)
        got = self.cswap(self.pick(w, 1 - self.c))
        w = self.pair(self.pick(w, self.c), got, self.c, 1)
        return w.reshape(4 * rows, cols)

    def collect(self, block):
        rows, cols = block.shape[0] // 4, block.shape[1]
        b = block.reshape(2, 2, rows, cols)
        keep = lax.dynamic_index_in_dim(b, self.c, 1, keepdims=False)
        give = lax.dynamic_index_in_dim(b, 1 - self.c, 1, keepdims=False)
        q = self.pair(keep, self.cswap(give), self.c, 1)
        got = self.yswap(self.pick(q, 1 - self.y))
        f = self.pair(self.pick(q, self.y), got, self.y, 0)
        return f.reshape(4, rows, cols)

    def gather_z(self, own, split):
        if self.nz != 4:
            blocks = [own]
            for k in range(1, self.nz):
                blocks.append(
                    self.zperm(own, [((t + k) % self.nz, t) for t in range(self.nz)])
                )
            return jnp.concatenate(blocks, 0)
        pairs_a = [(0, 1), (1, 0), (2, 3), (3, 2)]
        pairs_b = [(1, 2), (2, 1)]
        pairs_c = [(1, 0), (2, 3)]
        a = self.zperm(own, pairs_a)
        if split:
            b1 = self.zperm(own, pairs_b)
            b2 = self.zperm(a, pairs_b)
            c1 = self.zperm(b1, pairs_c)
            c2 = self.zperm(b2, pairs_c)
            return jnp.concatenate([own, a, b1 + c1, b2 + c2], 0)
        near = jnp.concatenate([own, a], 0)
        b = self.zperm(near, pairs_b)
        c = self.zperm(b, pairs_c)
        return jnp.concatenate([near, b + c], 0)

    def scatter_z(self, part, split):
        add = lambda p, q: (p.astype(F32) + q.astype(F32)).astype(BF)
        if self.nz != 4:
            total = part[0]
            for k in range(1, self.nz):
                total = add(
                    total,
                    self.zperm(part[k], [(t, (t + k) % self.nz) for t in range(self.nz)]),
                )
            return total
        pairs_a = [(0, 1), (1, 0), (2, 3), (3, 2)]
        pairs_b = [(1, 2), (2, 1)]
        pairs_c = [(0, 1), (3, 2)]
        own, near, o1, o2 = part
        if split:
            c2 = self.zperm(o2, pairs_c)
            c1 = self.zperm(o1, pairs_c)
            b2 = self.zperm(add(o2, c2), pairs_b)
            b1 = self.zperm(add(o1, c1), pairs_b)
        else:
            far = jnp.concatenate([o1, o2], 0)
            c = self.zperm(far, pairs_c)
            b = self.zperm(add(far, c), pairs_b)
            rows = own.shape[0]
            b1, b2 = b[:rows], b[rows:]
        a = self.zperm(add(near, b2), pairs_a)
        return (own.astype(F32) + b1.astype(F32) + a.astype(F32)).astype(BF)


def per_device(
    block_input,
    cotangent,
    seq_lengths,
    norm_attn_gain,
    norm_attn_shift,
    norm_mlp_gain,
    norm_mlp_shift,
    w_query,
    w_key,
    w_value,
    query_bias,
    key_bias,
    value_bias,
    w_attn_out,
    attn_out_bias,
    w_up,
    up_bias,
    w_down,
    down_bias,
):
    lk = Links()
    z, y, c = lk.z, lk.y, lk.c
    j = 2 * y + c
    toks, dim = block_input.shape
    rows = w_up.shape[0]
    heads_tensor = w_query.shape[1] // HEAD_DIM
    heads = heads_tensor // GROUP
    hcols = heads * HEAD_DIM
    units = w_up.shape[1] // GROUP
    zrows = GROUP * rows
    cuts = [(0, units // 2), (units // 2, units // 2)]

    def order_cols(a):
        return jnp.concatenate(
            [lax.dynamic_slice_in_dim(a, o * zrows, zrows, a.ndim - 1) for o in lk.order],
            a.ndim - 1,
        )

    def unorder_cols(a):
        if lk.nz == 4:
            inv = []
            for b in range(4):
                at = sum(jnp.where(o == b, i, 0) for i, o in enumerate(lk.order))
                inv.append(at)
        else:
            inv = [lax.rem(b - z + lk.nz, lk.nz) for b in range(lk.nz)]
        return jnp.concatenate(
            [lax.dynamic_slice_in_dim(a, o * zrows, zrows, a.ndim - 1) for o in inv],
            a.ndim - 1,
        )

    wdt = w_down.T
    wot = w_attn_out.T

    def owners(w):
        return jnp.transpose(w.reshape(rows, GROUP, -1), (1, 0, 2))

    up_o, down_o = owners(w_up), owners(wdt)
    attn_pieces = jnp.concatenate(
        [owners(w_query), owners(w_key), owners(w_value), owners(wot)], 2
    )
    mlp_pieces = [
        jnp.concatenate([up_o[:, :, s : s + f], down_o[:, :, s : s + f]], 2) for s, f in cuts
    ]

    m0 = lk.spread(mlp_pieces[0])
    wm0 = lk.gather_z(m0, True)

    grad_own = cotangent.astype(BF)
    lens_tile = jnp.pad(seq_lengths.astype(BF), ((0, 15), (0, dim - seq_lengths.shape[1])))
    payload = jnp.concatenate([order_cols(block_input), order_cols(grad_own), lens_tile], 0)
    t1 = lk.yswap(payload)
    t2 = lk.cswap(payload)
    t3 = lk.cswap(t1)
    parts = [payload, t1, t2, t3]
    xs = jnp.concatenate([p[:toks] for p in parts], 0).astype(F32)
    gr = jnp.concatenate([p[toks : 2 * toks] for p in parts], 0)
    lens = jnp.stack([p[2 * toks, : seq_lengths.shape[1]] for p in parts]).astype(jnp.int32)

    wa = lk.gather_z(lk.spread(attn_pieces), False)
    wm1 = lk.gather_z(lk.spread(mlp_pieces[1]), False)

    gains = order_cols(
        jnp.stack([norm_attn_gain, norm_attn_shift, norm_mlp_gain, norm_mlp_shift])
    )
    center = xs - jnp.mean(xs, axis=1, keepdims=True)
    inv_scale = lax.rsqrt(jnp.mean(center * center, axis=1, keepdims=True) + EPSILON)
    xhat = center * inv_scale
    attn_in = (xhat * gains[0] + gains[1]).astype(BF)
    mlp_in = (xhat * gains[2] + gains[3]).astype(BF)

    def blocks(g):
        return [g[i * zrows : (i + 1) * zrows] for i in range(lk.nz)]

    def mlp_slice(w, s, f):
        wu, wd = w[:, :f], w[:, f:]
        bias = lax.dynamic_slice_in_dim(up_bias, j * units + s, f, 0)
        up_pre = dot(mlp_in, wu) + bias
        act = gelu_value(up_pre).astype(BF)
        grad_up = dot(gr, wd) * gelu_slope(up_pre)
        bias_grad = jnp.sum(grad_up, axis=0)
        grad_up_b = grad_up.astype(BF)
        out = dot_nt(act, wd)
        gnorm = dot_nt(grad_up_b, wu)
        gw = jnp.concatenate([dot_tn(mlp_in, grad_up_b), dot_tn(gr, act)], 1).astype(BF)
        return out, gnorm, gw, bias_grad

    def attn_slice(w):
        wq, wk, wv, wo = (w[:, i * hcols : (i + 1) * hcols] for i in range(4))
        runs = GROUP
        shape = (runs, toks, heads, HEAD_DIM)
        cos, sin, allowed = jax.vmap(lambda l: layout(l, toks))(lens)
        cos, sin = cos[:, :, None, :], sin[:, :, None, :]
        qb = lax.dynamic_slice_in_dim(query_bias, j * hcols, hcols, 0)
        kb = lax.dynamic_slice_in_dim(key_bias, j * heads, heads, 0)
        vb = lax.dynamic_slice_in_dim(value_bias, j * hcols, hcols, 0)
        kb = jnp.pad(kb, ((0, 0), (0, HEAD_DIM - ROT)))
        q = rotate((dot(attn_in, wq) + qb).reshape(shape), cos, sin).astype(BF)
        k = rotate(dot(attn_in, wk).reshape(shape) + kb, cos, sin).astype(BF)
        v = (dot(attn_in, wv) + vb).astype(BF).reshape(shape)
        scale = 1.0 / math.sqrt(HEAD_DIM)
        mask = allowed[:, None]

        scores = jnp.einsum("rqhd,rkhd->rhqk", q, k, preferred_element_type=F32) * scale
        scores = jnp.where(mask, scores, MASKED_SCORE)
        top = jnp.max(scores, axis=3, keepdims=True)
        log_total = top + jnp.log(jnp.sum(jnp.exp(scores - top), axis=3, keepdims=True))
        probs = jnp.exp(scores - log_total)
        probs_b = probs.astype(BF)
        rows_o = jnp.einsum("rhqk,rkhd->rqhd", probs_b, v, preferred_element_type=F32).astype(BF)
        attn_rows = rows_o.reshape(runs * toks, hcols)
        out = dot_nt(attn_rows, wo)
        ga = dot(gr, wo).astype(BF)
        ga4 = ga.reshape(shape)
        delta = jnp.sum(ga4.astype(F32) * rows_o.astype(F32), axis=3)
        delta = jnp.transpose(delta, (0, 2, 1))
        gp = jnp.einsum("rqhd,rkhd->rhqk", ga4, v, preferred_element_type=F32)
        gs = (probs * (gp - delta[..., None])).astype(BF)
        gq = jnp.einsum("rhqk,rkhd->rqhd", gs, k, preferred_element_type=F32) * scale
        gk = jnp.einsum("rhqk,rqhd->rkhd", gs, q, preferred_element_type=F32) * scale
        gv = jnp.einsum("rhqk,rqhd->rkhd", probs_b, ga4, preferred_element_type=F32)
        gq = rotate(gq, cos, -sin).reshape(runs * toks, hcols)
        gk = rotate(gk, cos, -sin)
        gkb = jnp.sum(gk[..., :ROT], axis=(0, 1))
        gk = gk.reshape(runs * toks, hcols)
        gv = gv.reshape(runs * toks, hcols)
        gqb, gvb = jnp.sum(gq, axis=0), jnp.sum(gv, axis=0)
        gqkv = jnp.concatenate([gq, gk, gv], 1).astype(BF)
        gnorm = dot_nt(gqkv, w[:, : 3 * hcols])
        gw = jnp.concatenate([dot_tn(attn_in, gqkv), dot_tn(gr, attn_rows)], 1).astype(BF)
        return out, gnorm, gw, gqb, gkb, gvb

    out0, gn0, gw0, ub0 = mlp_slice(wm0, *cuts[0])
    r0 = lk.collect(lk.scatter_z(blocks(gw0), False))
    out_a, gna, gwa, gqb, gkb, gvb = attn_slice(wa)
    ra = lk.collect(lk.scatter_z(blocks(gwa), False))
    out1, gn1, gw1, ub1 = mlp_slice(wm1, *cuts[1])
    r1 = lk.collect(lk.scatter_z(blocks(gw1), True))
    gnm = gn0 + gn1

    def reduce_rows(a):
        a = a.astype(BF)
        half = a[: 2 * toks].astype(F32) + lk.cswap(a[2 * toks :]).astype(F32)
        got = lk.yswap(half[toks:].astype(BF))
        mine = (half[:toks] + got.astype(F32)).astype(BF)
        return mine.astype(F32) + lk.xswap(mine).astype(F32)

    mixed = reduce_rows(out0 + out_a + out1)
    block_output = (
        block_input.astype(F32) + unorder_cols(mixed) + attn_out_bias + down_bias
    )

    own_xhat, own_scale = xhat[:toks], inv_scale[:toks]
    g = reduce_rows(gna * gains[0] + gnm * gains[2])
    input_rows = own_scale * (
        g
        - jnp.mean(g, axis=1, keepdims=True)
        - own_xhat * jnp.mean(g * own_xhat, axis=1, keepdims=True)
    )
    input_grad = cotangent + unorder_cols(input_rows)

    norm_grads = jnp.stack(
        [
            jnp.sum(gna * xhat, axis=0),
            jnp.sum(gna, axis=0),
            jnp.sum(gnm * xhat, axis=0),
            jnp.sum(gnm, axis=0),
        ]
    )
    norm_grads = lax.psum(unorder_cols(norm_grads), ("dp", "tensor"))

    def place(v, total):
        return lax.dynamic_update_slice_in_dim(
            jnp.zeros((total,), F32), v, j * v.shape[0], 0
        )

    ub = jnp.concatenate([ub0, ub1])
    small = lax.psum(
        jnp.concatenate(
            [
                place(gqb, GROUP * hcols),
                place(gkb.reshape(-1), heads_tensor * ROT),
                place(gvb, GROUP * hcols),
                place(ub, GROUP * units),
                jnp.sum(cotangent, axis=0),
            ]
        ),
        "dp",
    )
    sizes = [GROUP * hcols, heads_tensor * ROT, GROUP * hcols, GROUP * units, dim]
    cut_at = [sum(sizes[:i]) for i in range(6)]
    s_q, s_k, s_v, s_u, s_o = (small[cut_at[i] : cut_at[i + 1]] for i in range(5))

    def join(f):
        return jnp.transpose(f, (1, 0, 2)).reshape(rows, -1)

    gq_w, gk_w, gv_w, go_w = (join(ra[:, :, i * hcols : (i + 1) * hcols]) for i in range(4))
    g_up = join(jnp.concatenate([r0[:, :, : cuts[0][1]], r1[:, :, : cuts[1][1]]], 2))
    g_down = join(jnp.concatenate([r0[:, :, cuts[0][1] :], r1[:, :, cuts[1][1] :]], 2))
    return (
        block_output,
        input_grad,
        norm_grads[0],
        norm_grads[1],
        norm_grads[2],
        norm_grads[3],
        gq_w.astype(F32),
        gk_w.astype(F32),
        gv_w.astype(F32),
        s_q,
        s_k.reshape(heads_tensor, ROT),
        s_v,
        go_w.astype(F32).T,
        s_o,
        g_up.astype(F32),
        s_u,
        g_down.astype(F32).T,
        s_o,
    )


def solution(mesh):
    in_specs = (
        P("dp", None),
        P("dp", None),
        P("dp", None),
        P(),
        P(),
        P(),
        P(),
        P("dp", "tensor"),
        P("dp", "tensor"),
        P("dp", "tensor"),
        P("tensor"),
        P("tensor", None),
        P("tensor"),
        P("tensor", "dp"),
        P(),
        P("dp", "tensor"),
        P("tensor"),
        P("tensor", "dp"),
        P(),
    )
    out_specs = (
        P("dp", None),
        P("dp", None),
        P(),
        P(),
        P(),
        P(),
        P("dp", "tensor"),
        P("dp", "tensor"),
        P("dp", "tensor"),
        P("tensor"),
        P("tensor", None),
        P("tensor"),
        P("tensor", "dp"),
        P(),
        P("dp", "tensor"),
        P("tensor"),
        P("tensor", "dp"),
        P(),
    )
    return jax.shard_map(
        per_device, mesh=mesh, in_specs=in_specs, out_specs=out_specs, check_vma=False
    )
```

```python
import functools
import math

import jax
import jax.numpy as jnp
from jax import lax
from jax.experimental import pallas as pl
from jax.experimental.pallas import tpu as pltpu
from jax.sharding import PartitionSpec as P

HEAD_DIM = 256
ROT = 64
BLOCK = 128
GROUP = 4

EPSILON = 1e-05
ROOT_HALF = 0.7071067811865476
DENSITY_SCALE = 0.3989422804014327
MASKED_SCORE = -1e30


BF = jnp.bfloat16
F32 = jnp.float32
ANY = pl.BlockSpec(memory_space=pl.ANY)
VM = pl.BlockSpec(memory_space=pltpu.VMEM)
SM = pl.BlockSpec(memory_space=pltpu.SMEM)


def sds(shape, dtype=BF):
    return jax.ShapeDtypeStruct(shape, dtype)


def dot(a, b):
    return jnp.dot(a, b, preferred_element_type=F32)


def dot_tn(a, b):
    return lax.dot_general(a, b, (((0,), (0,)), ((), ())), preferred_element_type=F32)


def dot_nt(a, b):
    return lax.dot_general(a, b, (((1,), (1,)), ((), ())), preferred_element_type=F32)


def after(value, *deps):
    return lax.optimization_barrier((value,) + deps)[0]


def mlp_tile(i, norm, gr, w, cols, bias, first_act, second_act, bias_sum):
    f = cols // 2
    up = dot(norm, w[:, :f]) + bias[0:1, :]
    e = 1.0 + lax.erf(up * ROOT_HALF)
    first_act[i] = (0.5 * up * e).astype(BF)
    slope = 0.5 * e + up * jnp.exp(-0.5 * up * up) * DENSITY_SCALE
    grad_up = dot(gr, w[:, f:]) * slope
    bias_sum[...] += jnp.sum(grad_up, axis=0, keepdims=True)
    second_act[i] = grad_up.astype(BF)
    out = dot_nt(first_act[i], w[:, f:])
    grad_norm = dot_nt(second_act[i], w[:, :f])
    return out, grad_norm


def turn(v, cos, sin):
    half = ROT // 2
    head = v[:, :128]
    lane = lax.broadcasted_iota(jnp.int32, head.shape, 1)
    other = jnp.where(lane < half, pltpu.roll(head, 128 - half, 1), pltpu.roll(head, half, 1))
    return jnp.concatenate([head * cos + other * sin, v[:, 128:]], axis=1)


def attn_tile(i, norm, gr, w, cols, bias, tables, rows_ref, grads_ref, bias_sum):
    cos_ref, sin_ref, segq_ref, segk_ref = tables
    hc = cols // 4
    toks = norm.shape[0]
    scale = 1.0 / math.sqrt(HEAD_DIM)
    cos, sin = cos_ref[i], sin_ref[i]
    segq, segk = segq_ref[i][:, 0:1], segk_ref[i][0:1, :]
    qi = lax.broadcasted_iota(jnp.int32, (toks, toks), 0)
    ki = lax.broadcasted_iota(jnp.int32, (toks, toks), 1)
    allowed = (ki <= qi) & (((segq == segk) & (segq >= 0)) | (ki == qi))
    qkv = dot(norm, w[:, : 3 * hc]) + bias[0:1, :]
    grad_attn = dot(gr, w[:, 3 * hc :]).astype(BF)
    for h in range(hc // HEAD_DIM):
        at = [slice(p * hc + h * HEAD_DIM, p * hc + (h + 1) * HEAD_DIM) for p in range(3)]
        mine = slice(h * HEAD_DIM, (h + 1) * HEAD_DIM)
        q = turn(qkv[:, at[0]], cos, sin).astype(BF)
        k = turn(qkv[:, at[1]], cos, sin).astype(BF)
        v = qkv[:, at[2]].astype(BF)
        scores = jnp.where(allowed, dot_nt(q, k) * scale, MASKED_SCORE)
        top = jnp.max(scores, axis=1, keepdims=True)
        log_total = top + jnp.log(jnp.sum(jnp.exp(scores - top), axis=1, keepdims=True))
        probs = jnp.exp(scores - log_total)
        probs_b = probs.astype(BF)
        rows = dot(probs_b, v).astype(BF)
        rows_ref[i, :, mine] = rows
        ga = grad_attn[:, mine]
        delta = jnp.sum(ga.astype(F32) * rows.astype(F32), axis=1, keepdims=True)
        gs = (probs * (dot_nt(ga, v) - delta)).astype(BF)
        gq = turn(dot(gs, k) * scale, cos, -sin)
        gk = turn(dot_tn(gs, q) * scale, cos, -sin)
        gv = dot_tn(probs_b, ga)
        for p, g in enumerate((gq, gk, gv)):
            bias_sum[0:1, at[p]] += jnp.sum(g, axis=0, keepdims=True)
            grads_ref[i, :, at[p]] = g.astype(BF)
    out = dot_nt(rows_ref[i], w[:, 3 * hc :])
    grad_norm = dot_nt(grads_ref[i], w[:, : 3 * hc])
    return out, grad_norm


def slice_kernel(attn, first, toks, *refs):
    n_tab = 4 if attn else 0
    w0, w1, wb, wc, t0, t1, t2, t3, gains, bias = refs[:10]
    tables = refs[10 : 10 + n_tab]
    refs = refs[10 + n_tab :]
    prev = [None, None, None, None]
    if not first:
        prev, refs = refs[:4], refs[4:]
    (own, near, far, keep_o, give_o, keep_g, give_g, sums, bias_sum) = refs[:9]
    (w, wcv, xg, norm, act1, act2, outv, gnv, gw, sem_w, sem_t, sem_p, sem_o, sem_g) = refs[9:]
    dim, cols = w.shape
    q = dim // 4
    copy = pltpu.make_async_copy
    cw = [
        copy(w0, w.at[pl.ds(0, q)], sem_w.at[0]),
        copy(w1, w.at[pl.ds(q, q)], sem_w.at[1]),
        copy(wb, w.at[pl.ds(2 * q, 2 * q)], sem_w.at[2]),
        copy(wc, wcv, sem_w.at[3]),
    ]
    ct = [
        copy(t.at[pl.ds(0, 2 * toks)], xg.at[i], sem_t.at[i])
        for i, t in enumerate((t0, t1, t2, t3))
    ]
    cp = []
    if not first:
        places = [outv.at[pl.ds(0, 2)], outv.at[pl.ds(2, 2)], gnv.at[pl.ds(0, 2)], gnv.at[pl.ds(2, 2)]]
        cp = [copy(s, t, sem_p.at[i]) for i, (s, t) in enumerate(zip(prev, places))]
    for k in [ct[0]] + cw + ct[1:] + cp:
        k.start()
    sums[...] = jnp.zeros_like(sums)
    bias_sum[...] = jnp.zeros_like(bias_sum)
    gain, shift = gains[0:1, :], gains[1:2, :]
    for i in range(4):
        ct[i].wait()
        if i == 0:
            for k in cw:
                k.wait()
            w[pl.ds(2 * q, 2 * q), :] = w[pl.ds(2 * q, 2 * q), :] + wcv[...]
            for k in cp:
                k.wait()
        x = xg[i, pl.ds(0, toks), :].astype(F32)
        center = x - jnp.mean(x, axis=1, keepdims=True)
        inv = lax.rsqrt(jnp.mean(center * center, axis=1, keepdims=True) + EPSILON)
        xhat = center * inv
        norm[i] = (xhat * gain + shift).astype(BF)
        gr = xg[i, pl.ds(toks, toks), :]
        if attn:
            out, grad = attn_tile(i, norm[i], gr, w, cols, bias, tables, act1, act2, bias_sum)
        else:
            out, grad = mlp_tile(i, norm[i], gr, w, cols, bias, act1, act2, bias_sum)
        sums[0:1, :] += jnp.sum(grad * xhat, axis=0, keepdims=True)
        sums[1:2, :] += jnp.sum(grad, axis=0, keepdims=True)
        grad = grad * gain
        if not first:
            out = out + outv[i].astype(F32)
            grad = grad + gnv[i].astype(F32)
        outv[i] = out.astype(BF)
        gnv[i] = grad.astype(BF)
    co = [
        copy(outv.at[pl.ds(0, 2)], keep_o, sem_o.at[0]),
        copy(outv.at[pl.ds(2, 2)], give_o, sem_o.at[1]),
        copy(gnv.at[pl.ds(0, 2)], keep_g, sem_o.at[2]),
        copy(gnv.at[pl.ds(2, 2)], give_g, sem_o.at[3]),
    ]
    for k in co:
        k.start()
    full = 4 * toks
    f1, f2 = act1.shape[2], act2.shape[2]
    a1 = act1[...].reshape(full, f1)
    a2 = act2[...].reshape(full, f2)
    dst = [own, near, far.at[0], far.at[1]]
    for b in (3, 2, 1, 0):
        at = slice(b * q, (b + 1) * q)
        gw[b, :, :f2] = dot_tn(norm[:, :, at].reshape(full, q), a2).astype(BF)
        gw[b, :, f2:] = dot_tn(xg[:, toks:, at].reshape(full, q), a1).astype(BF)
        k = copy(gw.at[b], dst[b], sem_g.at[b])
        k.start()
        co.append(k)
    for k in co:
        k.wait()


def slice_call(attn, toks, blocks, tiles, gains, bias, tables, prev, name):
    q, cols = blocks[0].shape
    dim = 4 * q
    f2 = 3 * cols // 4 if attn else cols // 2
    f1 = cols - f2
    first = prev is None
    half = (2, toks, dim)
    dma = pltpu.SemaphoreType.DMA
    return pl.pallas_call(
        functools.partial(slice_kernel, attn, first, toks),
        out_shape=[
            sds((q, cols)),
            sds((q, cols)),
            sds((2, q, cols)),
            sds(half),
            sds(half),
            sds(half),
            sds(half),
            sds((2, dim), F32),
            sds((1, f2), F32),
        ],
        in_specs=[ANY] * 8 + [VM] * (2 + len(tables)) + [ANY] * (0 if first else 4),
        out_specs=[ANY] * 7 + [VM, VM],
        scratch_shapes=[
            pltpu.VMEM((dim, cols), BF),
            pltpu.VMEM((2 * q, cols), BF),
            pltpu.VMEM((4, 2 * toks, dim), BF),
            pltpu.VMEM((4, toks, dim), BF),
            pltpu.VMEM((4, toks, f1), BF),
            pltpu.VMEM((4, toks, f2), BF),
            pltpu.VMEM((4, toks, dim), BF),
            pltpu.VMEM((4, toks, dim), BF),
            pltpu.VMEM((4, q, cols), BF),
        ]
        + [dma((4,))] * 5,
        compiler_params=pltpu.CompilerParams(vmem_limit_bytes=62 << 20),
        name=name,
        cost_estimate=pl.CostEstimate(
            flops=24 * toks * dim * cols, bytes_accessed=40 << 20, transcendentals=0
        ),
    )(
        *blocks[:2],
        blocks[2].reshape(2 * q, cols),
        blocks[3].reshape(2 * q, cols),
        *tiles,
        gains,
        bias,
        *tables,
        *(() if first else prev),
    )


def finish_kernel(bit, own, b, a, keep, give):
    total = (own[...].astype(F32) + b[0].astype(F32) + a[...].astype(F32)).astype(BF)
    rows = total.shape[0] // 2
    lo, hi = total[:rows], total[rows:]

    @pl.when(bit[0] == 0)
    def _():
        keep[0] = lo
        give[0] = hi

    @pl.when(bit[0] != 0)
    def _():
        keep[0] = hi
        give[0] = lo


def finish_call(own, b, a, c):
    q, cols = own.shape
    half = pl.BlockSpec((q // 2, cols), lambda i: (i, 0))
    piece = pl.BlockSpec((1, q // 4, cols), lambda i: (i, 0, 0))
    return pl.pallas_call(
        finish_kernel,
        grid=(2,),
        out_shape=[sds((2, q // 4, cols))] * 2,
        in_specs=[SM, half, pl.BlockSpec((1, q // 2, cols), lambda i: (0, i, 0)), half],
        out_specs=[piece, piece],
        name="finish",
        cost_estimate=pl.CostEstimate(flops=0, bytes_accessed=8 * q * cols, transcendentals=0),
    )(c, own, b, a)


def relay_kernel(bits, keep, got, send, stay):
    y, c = bits[0], bits[1]

    def put(y, c):
        send[c] = keep[1 - y]
        send[1 - c] = got[1 - y]
        stay[c] = keep[y]
        stay[1 - c] = got[y]

    for yy in range(2):
        for cc in range(2):
            pl.when((y == yy) & (c == cc))(functools.partial(put, yy, cc))


def relay_call(keep, got, bits):
    shape = sds(keep.shape)
    return pl.pallas_call(
        relay_kernel,
        out_shape=[shape, shape],
        in_specs=[SM, VM, VM],
        out_specs=[VM, VM],
        name="relay",
        cost_estimate=pl.CostEstimate(
            flops=0, bytes_accessed=8 * keep.size, transcendentals=0
        ),
    )(bits, keep, got)


class Links:
    def __init__(self):
        self.n = lax.axis_size("dp")
        self.nz = self.n // GROUP
        d = lax.axis_index("dp")
        self.z, self.y, self.c = d // 4, (d // 2) % 2, d % 2
        if self.nz == 4:
            low = self.z < 2
            self.order = [self.z, self.z ^ 1, jnp.where(low, 2, 1), jnp.where(low, 3, 0)]
        else:
            self.order = [lax.rem(self.z + k, self.nz) for k in range(self.nz)]

    def zperm(self, a, zpairs):
        return lax.ppermute(
            a, "dp", [(4 * s + j, 4 * t + j) for s, t in zpairs for j in range(4)]
        )

    def flip(self, a, bit):
        return lax.ppermute(a, "dp", [(d, d ^ bit) for d in range(self.n)])

    def yswap(self, a):
        return self.flip(a, 2)

    def cswap(self, a):
        return self.flip(a, 1)

    def xswap(self, a):
        t = lax.axis_size("tensor")
        return lax.ppermute(a, "tensor", [(i, t - 1 - i) for i in range(t)])

    def pick(self, a, i):
        return lax.dynamic_index_in_dim(a, i, 0, keepdims=False)

    def pair(self, own, other, bit, axis):
        return jnp.where(
            bit == 0, jnp.stack([own, other], axis), jnp.stack([other, own], axis)
        )

    def spread_y(self, pieces):
        rows, cols = pieces.shape[1:]
        p = pieces.reshape(2, 2, rows, cols)
        return self.pick(p, self.y), self.yswap(self.pick(p, 1 - self.y))

    def spread_c(self, mine, got):
        rows, cols = mine.shape[1:]
        w = self.pair(mine, got, self.y, 1)
        got = self.cswap(self.pick(w, 1 - self.c))
        w = self.pair(self.pick(w, self.c), got, self.c, 1)
        return w.reshape(4 * rows, cols)

    def gather_z(self, own):
        if self.nz != 4:
            blocks = [own]
            for k in range(1, self.nz):
                blocks.append(
                    self.zperm(own, [((t + k) % self.nz, t) for t in range(self.nz)])
                )
            w = jnp.concatenate(blocks, 0)
            q = w.shape[0] // 4
            far = w[2 * q :].reshape(2, q, -1)
            return [w[:q], w[q : 2 * q], far, jnp.zeros_like(far)]
        pairs_a = [(0, 1), (1, 0), (2, 3), (3, 2)]
        pairs_b = [(1, 2), (2, 1)]
        pairs_c = [(1, 0), (2, 3)]
        a = self.zperm(own, pairs_a)
        b = self.zperm(jnp.stack([own, a]), pairs_b)
        c = self.zperm(b, pairs_c)
        return [own, a, b, c]

    def scatter_z(self, own, near, far):
        add = lambda p, q: (p.astype(F32) + q.astype(F32)).astype(BF)
        if self.nz != 4:
            w = jnp.concatenate([own, near, far[0], far[1]], 0)
            part = w.reshape(self.nz, w.shape[0] // self.nz, w.shape[1])
            total = part[0]
            for k in range(1, self.nz):
                total = add(
                    total,
                    self.zperm(part[k], [(t, (t + k) % self.nz) for t in range(self.nz)]),
                )
            return total, jnp.zeros((2,) + total.shape, BF), jnp.zeros_like(total)
        pairs_a = [(0, 1), (1, 0), (2, 3), (3, 2)]
        pairs_b = [(1, 2), (2, 1)]
        pairs_c = [(0, 1), (3, 2)]
        c = self.zperm(far, pairs_c)
        b = self.zperm(add(far, c), pairs_b)
        a = self.zperm(add(near, b[1]), pairs_a)
        return own, b, a

    def all_sum(self, v):
        bit = 1
        while bit < self.n:
            v = v + self.flip(v, bit)
            bit *= 2
        return v


def per_device(
    block_input,
    cotangent,
    seq_lengths,
    norm_attn_gain,
    norm_attn_shift,
    norm_mlp_gain,
    norm_mlp_shift,
    w_query,
    w_key,
    w_value,
    query_bias,
    key_bias,
    value_bias,
    w_attn_out,
    attn_out_bias,
    w_up,
    up_bias,
    w_down,
    down_bias,
):
    lk = Links()
    z, y, c = lk.z, lk.y, lk.c
    j = 2 * y + c
    toks, dim = block_input.shape
    n_seq = seq_lengths.shape[1]
    rows = w_up.shape[0]
    heads_tensor = w_query.shape[1] // HEAD_DIM
    heads = heads_tensor // GROUP
    hcols = heads * HEAD_DIM
    units = w_up.shape[1] // GROUP
    zrows = GROUP * rows
    n_cut = 2
    f = units // n_cut
    bit_c = jnp.reshape(c, (1,)).astype(jnp.int32)
    bits = jnp.stack([y, c]).astype(jnp.int32)

    def order_cols(a):
        return jnp.concatenate(
            [lax.dynamic_slice_in_dim(a, o * zrows, zrows, a.ndim - 1) for o in lk.order],
            a.ndim - 1,
        )

    if lk.nz == 4:
        inverse = [sum(jnp.where(o == b, i, 0) for i, o in enumerate(lk.order)) for b in range(4)]
    else:
        inverse = [lax.rem(b - z + lk.nz, lk.nz) for b in range(lk.nz)]

    def unorder_cols(a):
        return jnp.concatenate(
            [lax.dynamic_slice_in_dim(a, o * zrows, zrows, a.ndim - 1) for o in inverse],
            a.ndim - 1,
        )

    def owners(w):
        return jnp.transpose(w.reshape(rows, GROUP, -1), (1, 0, 2))

    def mlp_pieces(s):
        up = w_up.reshape(rows, GROUP, n_cut, f)[:, :, s]
        down = w_down.reshape(GROUP, n_cut, f, rows)[:, s]
        return jnp.concatenate(
            [jnp.transpose(up, (1, 0, 2)), jnp.transpose(down, (0, 2, 1))], 2
        )

    attn_pieces = jnp.concatenate(
        [owners(w_query), owners(w_key), owners(w_value), owners(w_attn_out.T)], 2
    )

    m0 = lk.spread_y(mlp_pieces(0))
    wm0 = lk.gather_z(lk.spread_c(*m0))

    grad_own = cotangent.astype(BF)
    lens_tile = jnp.pad(seq_lengths.astype(BF), ((0, 15), (0, dim - n_seq)))
    payload = jnp.concatenate([order_cols(block_input), order_cols(grad_own), lens_tile], 0)
    payload = after(payload, m0[1])
    t1 = lk.yswap(payload)
    t2 = lk.cswap(payload)
    t3 = lk.cswap(t1)
    tiles = [payload, t1, t2, t3]

    pa = lk.spread_y(after(attn_pieces, t1))
    wa = lk.gather_z(after(lk.spread_c(*pa), wm0[1]))
    m1 = lk.spread_y(after(mlp_pieces(1), pa[1]))
    wm1 = lk.gather_z(after(lk.spread_c(*m1), wa[1]))

    gains = order_cols(
        jnp.stack([norm_attn_gain, norm_attn_shift, norm_mlp_gain, norm_mlp_shift])
    )

    lens = jnp.stack([p[2 * toks, :n_seq] for p in tiles]).astype(jnp.int32)
    padded = (lens + BLOCK - 1) // BLOCK * BLOCK
    starts = jnp.stack([jnp.sum(padded[:, :s], axis=1) for s in range(n_seq)], 1)
    slot = jnp.arange(toks, dtype=jnp.int32)[None, :, None]
    inside = (slot >= starts[:, None, :]) & (slot < (starts + lens)[:, None, :])
    number = jnp.arange(n_seq, dtype=jnp.int32)
    segment = jnp.sum(jnp.where(inside, number + 1, 0), axis=2) - 1
    position = jnp.sum(jnp.where(inside, slot - starts[:, None, :], 0), axis=2)
    lane = jnp.arange(128, dtype=jnp.int32)
    exponent = (2 * (lane % (ROT // 2))).astype(F32)
    frequency = jnp.where(lane < ROT, 10000.0 ** (-exponent / ROT), 0.0)
    angles = position.astype(F32)[:, :, None] * frequency
    cos = jnp.cos(angles)
    sin = jnp.where(lane < ROT // 2, -jnp.sin(angles), jnp.sin(angles))
    segq = jnp.broadcast_to(segment[:, :, None], (GROUP, toks, 128))
    segk = jnp.broadcast_to(segment[:, None, :], (GROUP, 8, toks))
    tables = (cos, sin, segq, segk)

    def mlp_bias(s):
        return lax.dynamic_slice_in_dim(up_bias, j * units + s * f, f, 0)[None, :]

    key_full = jnp.pad(key_bias, ((0, 0), (0, HEAD_DIM - ROT)))
    attn_bias = jnp.concatenate(
        [
            lax.dynamic_slice_in_dim(v, j * hcols, hcols, 0)
            for v in (query_bias, key_full.reshape(-1), value_bias)
        ]
    )[None, :]

    def collect(own, b, a):
        keep, give = finish_call(own, b, a, bit_c)
        send, stay = relay_call(keep, lk.cswap(give), bits)
        return stay, lk.yswap(send)

    r_m0 = slice_call(False, toks, wm0, tiles, gains[2:], mlp_bias(0), (), None, "mlp0")
    r_a = slice_call(True, toks, wa, tiles, gains[:2], attn_bias, tables, r_m0[3:7], "attn")
    r_m1 = slice_call(False, toks, wm1, tiles, gains[2:], mlp_bias(1), (), r_a[3:7], "mlp1")
    e_m0 = collect(*lk.scatter_z(*r_m0[:3]))
    e_a = collect(*lk.scatter_z(*r_a[:3]))
    e_m1 = collect(*lk.scatter_z(*r_m1[:3]))

    def reduce_rows(keep, give):
        got = lk.cswap(give)
        give_y = (keep[1].astype(F32) + got[1].astype(F32)).astype(BF)
        got_y = lk.yswap(give_y)
        mine = (keep[0].astype(F32) + got[0].astype(F32) + got_y.astype(F32)).astype(BF)
        return mine.astype(F32) + lk.xswap(mine).astype(F32)

    mixed = reduce_rows(r_m1[3], r_m1[4])
    block_output = (
        block_input.astype(F32) + unorder_cols(mixed) + attn_out_bias + down_bias
    )

    source = block_input.astype(F32)
    center = source - jnp.mean(source, axis=1, keepdims=True)
    inv_scale = lax.rsqrt(jnp.mean(center * center, axis=1, keepdims=True) + EPSILON)
    xhat = center * inv_scale
    g = unorder_cols(reduce_rows(r_m1[5], r_m1[6]))
    input_grad = cotangent + inv_scale * (
        g
        - jnp.mean(g, axis=1, keepdims=True)
        - xhat * jnp.mean(g * xhat, axis=1, keepdims=True)
    )

    def place(v, total):
        return lax.dynamic_update_slice_in_dim(jnp.zeros((total,), F32), v, j * v.shape[0], 0)

    ub = jnp.concatenate([r_m0[8][0], r_m1[8][0]])
    qkv_sums = r_a[8][0]
    key_sums = qkv_sums[hcols : 2 * hcols].reshape(heads, HEAD_DIM)[:, :ROT].reshape(-1)
    parts = [
        unorder_cols(r_a[7]).reshape(-1),
        unorder_cols(r_m0[7] + r_m1[7]).reshape(-1),
        place(qkv_sums[:hcols], GROUP * hcols),
        place(key_sums, heads_tensor * ROT),
        place(qkv_sums[2 * hcols :], GROUP * hcols),
        place(ub, GROUP * units),
        jnp.sum(cotangent, axis=0),
    ]
    sizes = [p.shape[0] for p in parts]
    small = lk.all_sum(jnp.concatenate(parts).reshape(-1, 128))
    norm_rows = 4 * dim // 128
    norm_sums = small[:norm_rows]
    norm_sums = (norm_sums + lk.xswap(norm_sums)).reshape(4, dim)
    small = small.reshape(-1)
    cut_at = [sum(sizes[:i]) for i in range(8)]
    s_q, s_k, s_v, s_u, s_o = (small[cut_at[i] : cut_at[i + 1]] for i in range(2, 7))

    def join(ends, lo, hi):
        stay, got = ends
        return lk.pair(stay[:, :, lo:hi], got[:, :, lo:hi], y, 0).reshape(
            GROUP, rows, hi - lo
        )

    def by_cols(p):
        return jnp.transpose(p, (1, 0, 2)).reshape(rows, -1).astype(F32)

    gq_w, gk_w, gv_w = (by_cols(join(e_a, i * hcols, (i + 1) * hcols)) for i in range(3))
    go_w = join(e_a, 3 * hcols, 4 * hcols)
    go_w = jnp.transpose(go_w, (0, 2, 1)).reshape(-1, rows).astype(F32)
    ups = jnp.stack([join(e, 0, f) for e in (e_m0, e_m1)], 2)
    downs = jnp.stack([join(e, f, 2 * f) for e in (e_m0, e_m1)], 1)
    g_up = jnp.transpose(ups, (1, 0, 2, 3)).reshape(rows, -1).astype(F32)
    g_down = jnp.transpose(downs, (0, 1, 3, 2)).reshape(-1, rows).astype(F32)
    return (
        block_output,
        input_grad,
        norm_sums[0],
        norm_sums[1],
        norm_sums[2],
        norm_sums[3],
        gq_w,
        gk_w,
        gv_w,
        s_q,
        s_k.reshape(heads_tensor, ROT),
        s_v,
        go_w,
        s_o,
        g_up,
        s_u,
        g_down,
        s_o,
    )
def solution(mesh):
    in_specs = (
        P("dp", None),
        P("dp", None),
        P("dp", None),
        P(),
        P(),
        P(),
        P(),
        P("dp", "tensor"),
        P("dp", "tensor"),
        P("dp", "tensor"),
        P("tensor"),
        P("tensor", None),
        P("tensor"),
        P("tensor", "dp"),
        P(),
        P("dp", "tensor"),
        P("tensor"),
        P("tensor", "dp"),
        P(),
    )
    out_specs = (
        P("dp", None),
        P("dp", None),
        P(),
        P(),
        P(),
        P(),
        P("dp", "tensor"),
        P("dp", "tensor"),
        P("dp", "tensor"),
        P("tensor"),
        P("tensor", None),
        P("tensor"),
        P("tensor", "dp"),
        P(),
        P("dp", "tensor"),
        P("tensor"),
        P("tensor", "dp"),
        P(),
    )
    return jax.shard_map(
        per_device, mesh=mesh, in_specs=in_specs, out_specs=out_specs, check_vma=False
    )
```
